32 devices in a mesh: depth: 2 (over core), lat: 16 (over z, y, x).
Axes of the slice: x: 2, y: 2, z: 4, core: 2. Of those that a mesh axis runs over, the one named last changes fastest.
Arguments:
- fields: float32 [6, 96, 16, 512], P(None, 'lat', 'depth'), may hold values from -3 to 3
- material: int32 [96, 16, 512], P('lat', 'depth'), may hold values from 0 to 3
- source_mask: int32 [96, 16, 512], P('lat', 'depth'), may hold values 0 or 1
- eps_table: float32 [4], replicated, may hold values from 1 to 6
- kerr_table: float32 [4], replicated, may hold values from 0.3 to 3
Outputs:
- fields_out: float32 [6, 96, 16, 512], P(None, 'lat', 'depth')
- image: float32 [96, 8, 512], P('lat', None, 'depth')
The draws below stay inside these ranges and needn't reach their ends.
Inputs may be any that keep to these rules, and one draw needn't show every extreme that they name: material indexes the tables.
All inputs are finite; a program needn't handle non-finite values. No bound on the sum of `source_mask` on one device may be relied on, other than what follows from the above.
Results may differ from the reference program's by a relative error of at most 0.0003.
Values sent between devices are 32-bit elements; how exact they have to be, the bound alone decides.
No kernel may reach another device: no remote copies, remote signals or barrier semaphores. Data moves between devices by JAX's collectives and lax.ppermute only.
A program may use at most 64 MiB of HBM per device.

```python
import math
import jax
import jax.numpy as jnp
from jax import lax

NY = 512
STEPS = 16
MATERIALS = 4
NX = 96
NZ = 16


def set_ends(array, own_key, smallest, high):
    dims = array.shape
    place = [jax.random.randint(jax.random.fold_in(own_key, axis), (), 0, dims[axis]) for axis in range(len(dims))]
    array = array.at[tuple(place)].set(smallest)
    longest = dims.index(max(dims))
    place[longest] = (place[longest] + 1) % dims[longest]
    return array.at[tuple(place)].set(high)


def steps_of(own_key, dims, pieces, low, top_value):
    def one(axis_at, parts):
        draws = jax.random.uniform(jax.random.fold_in(jax.random.fold_in(own_key, 6), axis_at), (parts,), jnp.float32, low / len(pieces), top_value / len(pieces))
        return jnp.repeat(jnp.exp(draws), dims[axis_at] // parts).reshape((-1,) + (1,) * (len(dims) - axis_at - 1))

    factor_of = one(*pieces[0])
    for cut in pieces[1:]:
        factor_of = factor_of * one(*cut)
    return factor_of


def centred(own_key, dims, deviation, limit, split=(), kind=jnp.bfloat16):
    entries = deviation * jax.random.normal(own_key, dims, jnp.float32)
    if split:
        entries = entries * steps_of(own_key, dims, split, -0.22, 0.18)
    return jnp.clip(entries, -limit, limit).astype(kind)


def setup_inputs(seed: int = 0) -> dict:
    arg_keys = jax.random.split(jax.random.key(seed), 6)
    return {
        "fields": centred(arg_keys[0], (6, NX, NZ, NY), 0.5, 3.0, ((1, 16), (2, 2)), jnp.float32),
        "material": set_ends(jax.random.randint(arg_keys[1], (NX, NZ, NY), 0, MATERIALS), jax.random.fold_in(arg_keys[1], 1), 0, MATERIALS - 1).astype(jnp.int32),
        "source_mask": set_ends((jax.random.randint(arg_keys[2], (NX, NZ, NY), 0, 8) < 1).astype(jnp.int32), jax.random.fold_in(arg_keys[2], 1), 0, 1),
        "eps_table": jnp.clip(jax.random.uniform(arg_keys[3], (MATERIALS,), jnp.float32, 1.0, 6.0), 1.0, 6.0),
        "kerr_table": jnp.clip(jnp.exp(jax.random.uniform(arg_keys[4], (MATERIALS,), jnp.float32, math.log(0.3), math.log(3.0))), 0.3, 3.0),
    }


COURANT = 0.55
OMEGAS = (0.9, 1.3)
SOURCE_AMP = 1.0
QUARTERS = (3, 5)
HIGHEST = lax.Precision.HIGHEST

def forward_diff(field, along):
    length = field.shape[along]
    ahead = lax.slice_in_dim(field, 1, length, axis=along)
    ahead = jnp.concatenate([ahead, jnp.zeros_like(lax.slice_in_dim(field, 0, 1, axis=along))], axis=along)
    return ahead - field

def backward_diff(field, along):
    length = field.shape[along]
    behind = lax.slice_in_dim(field, 0, length - 1, axis=along)
    behind = jnp.concatenate([jnp.zeros_like(lax.slice_in_dim(field, 0, 1, axis=along)), behind], axis=along)
    return field - behind

def drive(moment):
    middle = moment + 0.5
    return SOURCE_AMP * (jnp.sin(OMEGAS[0] * middle) + jnp.sin(OMEGAS[1] * middle))

def yee_step(fields, permittivity, kerr_coef, source_flag, inside, pulse):
    elec_x, elec_y, elec_z = (fields[0], fields[1], fields[2])
    magn_x, magn_y, magn_z = (fields[3], fields[4], fields[5])
    magn_x = (magn_x - COURANT * (forward_diff(elec_z, 2) - forward_diff(elec_y, 1))) * inside
    magn_y = (magn_y - COURANT * (forward_diff(elec_x, 1) - forward_diff(elec_z, 0))) * inside
    magn_z = (magn_z - COURANT * (forward_diff(elec_y, 0) - forward_diff(elec_x, 2))) * inside
    energy = elec_x * elec_x + elec_y * elec_y + elec_z * elec_z
    factor = COURANT / (permittivity + kerr_coef * energy)
    new_x = (elec_x + factor * (backward_diff(magn_z, 2) - backward_diff(magn_y, 1)) + source_flag * pulse) * inside
    new_y = (elec_y + factor * (backward_diff(magn_x, 1) - backward_diff(magn_z, 0))) * inside
    new_z = (elec_z + factor * (backward_diff(magn_y, 0) - backward_diff(magn_x, 2))) * inside
    return jnp.stack([new_x, new_y, new_z, magn_x, magn_y, magn_z])

def lookup(material, table):
    result = jnp.zeros(material.shape, jnp.float32)
    for level in range(table.shape[0]):
        result = jnp.where(material == level, table[level], result)
    return result

def accumulate(spectrum, plane, moment):
    later = moment + 1.0
    trig = jnp.stack([jnp.stack([jnp.cos(omega * later), -jnp.sin(omega * later)]) for omega in OMEGAS])
    return spectrum + trig[:, None, :, None, None] * plane[None, :, None, :, :]

def chirp(row_index, col_index, length):
    gap = row_index[:, None] - col_index[None, :]
    squared = gap * gap
    reals, imags = ([], [])
    for quarter in QUARTERS:
        wrapped = quarter * squared % (8 * length)
        phase = wrapped.astype(jnp.float32) * (math.pi / (4.0 * length))
        reals.append(jnp.cos(phase) / math.sqrt(length))
        imags.append(jnp.sin(phase) / math.sqrt(length))
    return (jnp.stack(reals), jnp.stack(imags))

def column_transform(real, imag, y_real, y_imag):
    v_real = jnp.einsum('fcxy,fyk->fcxk', real, y_real, precision=HIGHEST) - jnp.einsum('fcxy,fyk->fcxk', imag, y_imag, precision=HIGHEST)
    v_imag = jnp.einsum('fcxy,fyk->fcxk', real, y_imag, precision=HIGHEST) + jnp.einsum('fcxy,fyk->fcxk', imag, y_real, precision=HIGHEST)
    return (v_real, v_imag)

def row_transform(x_real, x_imag, v_real, v_imag):
    w_real = jnp.einsum('fix,fcxk->ifck', x_real, v_real, precision=HIGHEST) - jnp.einsum('fix,fcxk->ifck', x_imag, v_imag, precision=HIGHEST)
    w_imag = jnp.einsum('fix,fcxk->ifck', x_real, v_imag, precision=HIGHEST) + jnp.einsum('fix,fcxk->ifck', x_imag, v_real, precision=HIGHEST)
    return jnp.stack([w_real, w_imag], axis=3)

def reference(fields, material, source_mask, eps_table, kerr_table):
    permittivity = lookup(material, eps_table)
    kerr_coef = lookup(material, kerr_table)
    source_flag = source_mask.astype(jnp.float32)
    spectrum = jnp.zeros((2, 2, 2, NX, NY), jnp.float32)
    for step in range(STEPS):
        moment = jnp.float32(step)
        fields = yee_step(fields, permittivity, kerr_coef, source_flag, 1.0, drive(moment))
        spectrum = accumulate(spectrum, fields[0:2, :, NZ - 1, :], moment)
    y_index = jnp.arange(NY, dtype=jnp.int32)
    x_index = jnp.arange(NX, dtype=jnp.int32)
    y_real, y_imag = chirp(y_index, y_index, NY)
    x_real, x_imag = chirp(x_index, x_index, NX)
    v_real, v_imag = column_transform(spectrum[:, :, 0], spectrum[:, :, 1], y_real, y_imag)
    image = row_transform(x_real, x_imag, v_real, v_imag)
    return (fields, image.reshape(NX, 8, NY))
```

```python
import functools
import math

import jax
import jax.numpy as jnp
from jax import lax
from jax.experimental import pallas as pl
from jax.experimental.pallas import tpu as pltpu
from jax.sharding import PartitionSpec as P

STEPS = 16
HALO_STEPS = 4


COURANT = 0.55
OMEGAS = (0.9, 1.3)
SOURCE_AMP = 1.0
QUARTERS = (3, 5)
HIGHEST = lax.Precision.HIGHEST


def padded_2(block, sides, width):
    for axis, dim in sides:
        count = lax.axis_size(axis)
        forward = [(i, i + 1) for i in range(count - 1)]
        backward = [(target, source) for source, target in forward]
        low = lax.ppermute(
            lax.slice_in_dim(block, block.shape[dim] - width, None, axis=dim), axis, forward
        )
        high = lax.ppermute(lax.slice_in_dim(block, 0, width, axis=dim), axis, backward)
        block = jnp.concatenate([low, block, high], axis=dim)
    return block


def from_root(block, axis, owner):
    block = jnp.where(lax.axis_index(axis) == owner, block, jnp.zeros_like(block))
    return lax.psum(block, axis)


def forward_diff(field, along):
    length = field.shape[along]
    ahead = lax.slice_in_dim(field, 1, length, axis=along)
    ahead = jnp.concatenate(
        [ahead, jnp.zeros_like(lax.slice_in_dim(field, 0, 1, axis=along))], axis=along
    )
    return ahead - field


def backward_diff(field, along):
    length = field.shape[along]
    behind = lax.slice_in_dim(field, 0, length - 1, axis=along)
    behind = jnp.concatenate(
        [jnp.zeros_like(lax.slice_in_dim(field, 0, 1, axis=along)), behind], axis=along
    )
    return field - behind


def drive(moment):
    middle = moment + 0.5
    return SOURCE_AMP * (jnp.sin(OMEGAS[0] * middle) + jnp.sin(OMEGAS[1] * middle))


def yee_step(fields, permittivity, kerr_coef, source_flag, inside, pulse):
    elec_x, elec_y, elec_z = (fields[0], fields[1], fields[2])
    magn_x, magn_y, magn_z = (fields[3], fields[4], fields[5])
    magn_x = (magn_x - COURANT * (forward_diff(elec_z, 2) - forward_diff(elec_y, 1))) * inside
    magn_y = (magn_y - COURANT * (forward_diff(elec_x, 1) - forward_diff(elec_z, 0))) * inside
    magn_z = (magn_z - COURANT * (forward_diff(elec_y, 0) - forward_diff(elec_x, 2))) * inside
    energy = elec_x * elec_x + elec_y * elec_y + elec_z * elec_z
    factor = COURANT / (permittivity + kerr_coef * energy)
    new_x = (
        elec_x
        + factor * (backward_diff(magn_z, 2) - backward_diff(magn_y, 1))
        + source_flag * pulse
    ) * inside
    new_y = (elec_y + factor * (backward_diff(magn_x, 1) - backward_diff(magn_z, 0))) * inside
    new_z = (elec_z + factor * (backward_diff(magn_y, 0) - backward_diff(magn_x, 2))) * inside
    return jnp.stack([new_x, new_y, new_z, magn_x, magn_y, magn_z])


def lookup(material, table):
    result = jnp.zeros(material.shape, jnp.float32)
    for level in range(table.shape[0]):
        result = jnp.where(material == level, table[level], result)
    return result


def accumulate(spectrum, plane, moment):
    later = moment + 1.0
    trig = jnp.stack(
        [jnp.stack([jnp.cos(omega * later), -jnp.sin(omega * later)]) for omega in OMEGAS]
    )
    return spectrum + trig[:, None, :, None, None] * plane[None, :, None, :, :]


def chirp(row_index, col_index, length):
    gap = row_index[:, None] - col_index[None, :]
    squared = gap * gap
    reals, imags = ([], [])
    for quarter in QUARTERS:
        wrapped = quarter * squared % (8 * length)
        phase = wrapped.astype(jnp.float32) * (math.pi / (4.0 * length))
        reals.append(jnp.cos(phase) / math.sqrt(length))
        imags.append(jnp.sin(phase) / math.sqrt(length))
    return (jnp.stack(reals), jnp.stack(imags))


def column_transform(real, imag, y_real, y_imag):
    v_real = jnp.einsum("fcxy,fyk->fcxk", real, y_real, precision=HIGHEST) - jnp.einsum(
        "fcxy,fyk->fcxk", imag, y_imag, precision=HIGHEST
    )
    v_imag = jnp.einsum("fcxy,fyk->fcxk", real, y_imag, precision=HIGHEST) + jnp.einsum(
        "fcxy,fyk->fcxk", imag, y_real, precision=HIGHEST
    )
    return (v_real, v_imag)


def row_transform(x_real, x_imag, v_real, v_imag):
    w_real = jnp.einsum("fix,fcxk->ifck", x_real, v_real, precision=HIGHEST) - jnp.einsum(
        "fix,fcxk->ifck", x_imag, v_imag, precision=HIGHEST
    )
    w_imag = jnp.einsum("fix,fcxk->ifck", x_real, v_imag, precision=HIGHEST) + jnp.einsum(
        "fix,fcxk->ifck", x_imag, v_real, precision=HIGHEST
    )
    return jnp.stack([w_real, w_imag], axis=3)


def local_general(fields, material, source_mask, eps_table, kerr_table):
    width_x = fields.shape[1]
    depth_z = fields.shape[2]
    span_y = fields.shape[3]
    lat_count = lax.axis_size("lat")
    depth_count = lax.axis_size("depth")
    total_x = width_x * lat_count
    total_z = depth_z * depth_count
    lat_pos = lax.axis_index("lat")
    depth_pos = lax.axis_index("depth")
    coefs = jnp.stack(
        [lookup(material, eps_table), lookup(material, kerr_table), source_mask.astype(jnp.float32)]
    )
    empty_spectrum = jnp.zeros((2, 2, 2, width_x, span_y), jnp.float32)
    coef_pad = padded_2(coefs, (("depth", 2), ("lat", 1)), HALO_STEPS)
    place_x = lat_pos * width_x - HALO_STEPS + jnp.arange(width_x + 2 * HALO_STEPS, dtype=jnp.int32)
    place_z = (
        depth_pos * depth_z - HALO_STEPS + jnp.arange(depth_z + 2 * HALO_STEPS, dtype=jnp.int32)
    )
    valid_x = (place_x >= 0) & (place_x < total_x)
    valid_z = (place_z >= 0) & (place_z < total_z)
    valid = valid_x[:, None] & valid_z[None, :]
    setup_inside = valid.astype(jnp.float32)[:, :, None]
    setup_permittivity = jnp.where(valid[:, :, None], coef_pad[0], 1.0)
    kerr_coef = coef_pad[1]
    source_flag = coef_pad[2]

    def one_block(block, carry):
        state, spectrum = carry
        padded = padded_2(state, (("depth", 2), ("lat", 1)), HALO_STEPS)
        for inner in range(HALO_STEPS):
            moment = (block * HALO_STEPS + inner).astype(jnp.float32)
            padded = yee_step(
                padded, setup_permittivity, kerr_coef, source_flag, setup_inside, drive(moment)
            )
            plane = padded[0:2, HALO_STEPS : HALO_STEPS + width_x, HALO_STEPS + depth_z - 1, :]
            spectrum = accumulate(spectrum, plane, moment)
        state = padded[:, HALO_STEPS : HALO_STEPS + width_x, HALO_STEPS : HALO_STEPS + depth_z]
        return (state, spectrum)

    state, spectrum = lax.fori_loop(0, STEPS // HALO_STEPS, one_block, (fields, empty_spectrum))
    spectrum = from_root(spectrum, "depth", depth_count - 1)
    col_count = span_y // depth_count
    col_index = depth_pos * col_count + jnp.arange(col_count, dtype=jnp.int32)
    y_real, y_imag = chirp(jnp.arange(span_y, dtype=jnp.int32), col_index, span_y)
    v_real, v_imag = column_transform(spectrum[:, :, 0], spectrum[:, :, 1], y_real, y_imag)
    row_local = lat_pos * width_x + jnp.arange(width_x, dtype=jnp.int32)
    row_index = jnp.arange(width_x * lax.axis_size("lat"), dtype=jnp.int32)
    x_real, x_imag = chirp(row_index, row_local, total_x)
    image = lax.psum_scatter(
        row_transform(x_real, x_imag, v_real, v_imag), "lat", scatter_dimension=0, tiled=True
    )
    return (state, image.reshape(width_x, 8, col_count))


GROUP = 4
LANES = 128
SUBS = 8
PER_TILE = 4
VMEM = pl.BlockSpec(memory_space=pltpu.VMEM)
SMEM = pl.BlockSpec(memory_space=pltpu.SMEM)


def place():
    lat_pos = lax.axis_index("lat")
    return lat_pos // GROUP, lat_pos % GROUP, lax.axis_index("depth")


def call(body, out_shape, operands, in_specs=None, scratch=(), name=None):
    return pl.pallas_call(
        body,
        out_shape=out_shape,
        in_specs=in_specs or [VMEM] * len(operands),
        out_specs=jax.tree.map(lambda _: VMEM, out_shape),
        scratch_shapes=list(scratch),
        compiler_params=pltpu.CompilerParams(vmem_limit_bytes=56 * 1024 * 1024),
        name=name,
    )(*operands)


def f32(*shape):
    return jax.ShapeDtypeStruct(shape, jnp.float32)


def lane_iota(rows=SUBS):
    return lax.broadcasted_iota(jnp.int32, (rows, LANES), 1)


def quarters_body(pos, fields, material, mask, *pieces):
    width_x = fields.shape[1]
    lane = lane_iota()
    _, member, _ = pos()
    halo = STEPS

    def row(r, _):
        for j in range(GROUP):
            quarter = member ^ j
            left = jnp.maximum(quarter - 1, 0)
            right = jnp.minimum(quarter + 1, GROUP - 1)
            has_left = jnp.where(quarter > 0, 1.0, 0.0)
            has_right = jnp.where(quarter < GROUP - 1, 1.0, 0.0)
            keep = jnp.where(lane >= LANES // 2, has_left, has_right)

            def read(a, block):
                cols = pl.ds(pl.multiple_of(block * LANES, LANES), LANES)
                if a < 6:
                    return fields[a, r, :, cols]
                source = material if a == 6 else mask
                return source[r, :, cols].astype(jnp.float32)

            for g in range(8 // PER_TILE):
                packed = jnp.zeros((SUBS, LANES), jnp.float32)
                for k in range(PER_TILE):
                    a = g * PER_TILE + k
                    pieces[j][r, a] = read(a, quarter)
                    edge = jnp.where(lane >= LANES // 2, read(a, left), read(a, right)) * keep
                    edge = pltpu.roll(edge, (2 * halo * k + halo) % LANES, 1)
                    packed = jnp.where(lane // (2 * halo) == k, edge, packed)
                pieces[j][r, 8 + g] = packed
        return 0

    lax.fori_loop(0, width_x, row, 0)


def gather_rows_body(pos, p0, p1, p2, p3, own, up, down):
    _, member, _ = pos()
    width_x = p0.shape[0]
    rows = GROUP * width_x
    for j, piece in enumerate((p0, p1, p2, p3)):
        first = (member ^ j) * width_x
        for r in range(width_x):
            own[first + r] = piece[r]
    for r in range(STEPS):
        up[r] = own[rows - STEPS + r]
        down[r] = own[r]


def window_tile(packed, r, a, core, lane):
    half = LANES // 2
    halo = STEPS
    main = pltpu.roll(packed[r, a], (halo + half * core) % LANES, 1)
    edge = pltpu.roll(
        packed[r, 8 + a // PER_TILE], (half * core + LANES - 2 * halo * (a % PER_TILE)) % LANES, 1
    )
    below = jnp.where(core == 0, halo, 0)
    above = jnp.where(core == 0, LANES, half + halo)
    return jnp.where((lane < below) | (lane >= above), edge, main)


def windows_body(pos, packed, out):
    _, _, core = pos()
    lane = lane_iota()

    def row(r, _):
        for a in range(8):
            out[r, a] = window_tile(packed, r, a, 1 - core, lane)
        return 0

    lax.fori_loop(0, packed.shape[0], row, 0)


def windows2_body(pos, low, high, out):
    _, _, core = pos()
    lane = lane_iota()

    def row(r, _):
        for a in range(8):
            out[r, a] = window_tile(low, r, a, 1 - core, lane)
            out[STEPS + r, a] = window_tile(high, r, a, 1 - core, lane)
        return 0

    lax.fori_loop(0, STEPS, row, 0)


def trig_of(step):
    later = step + 1.0
    return [[math.cos(omega * later), -math.sin(omega * later)] for omega in OMEGAS]


def steps_body(
    pos, total_x, total_y, eps, kerr, own, low, high, theirs, theirs_halo,
    mine_out, send_out, spec_out, field, coef, hist,
):
    group, member, core = pos()
    lane = lane_iota()
    half = LANES // 2
    halo = STEPS
    rows = own.shape[0]
    span = rows + 2 * halo
    depth = 2 * SUBS
    levels = eps.shape[0]

    def put(row, core_at, tiles):
        subs = pl.ds(pl.multiple_of(core_at * SUBS, SUBS), SUBS)
        for a in range(6):
            field[row, a, subs, :] = tiles[a]
        eps_of = jnp.zeros((SUBS, LANES), jnp.float32)
        kerr_of = jnp.zeros((SUBS, LANES), jnp.float32)
        for level in range(levels):
            hit = tiles[6] == float(level)
            eps_of = jnp.where(hit, eps[level], eps_of)
            kerr_of = jnp.where(hit, kerr[level], kerr_of)
        coef[row, 0, subs, :] = eps_of
        coef[row, 1, subs, :] = kerr_of
        coef[row, 2, subs, :] = tiles[7]

    def fill(packed, at, count, other, other_at):
        def row(r, _):
            put(at + r, core, [window_tile(packed, r, a, core, lane) for a in range(8)])
            put(at + r, 1 - core, [other[other_at + r, a] for a in range(8)])
            return 0

        lax.fori_loop(0, count, row, 0)

    fill(own, halo, rows, theirs, 0)
    fill(low, 0, halo, theirs_halo, 0)
    fill(high, halo + rows, halo, theirs_halo, halo)

    lane2 = lane_iota(depth)
    sub2 = lax.broadcasted_iota(jnp.int32, (depth, LANES), 0)
    at_y = member * LANES + core * half - halo + lane2
    in_y = jnp.where((at_y >= 0) & (at_y < total_y), COURANT, 0.0)
    not_top = sub2 < depth - 1
    not_low = sub2 > 0

    def next_y(f):
        return pltpu.roll(f, LANES - 1, 1)

    def prev_y(f):
        return pltpu.roll(f, 1, 1)

    def next_z(f):
        return jnp.where(not_top, pltpu.roll(f, depth - 1, 0), 0.0)

    def prev_z(f):
        return jnp.where(not_low, pltpu.roll(f, 1, 0), 0.0)

    first_x = group * rows - halo

    def step(n, _):
        middle = n.astype(jnp.float32) + 0.5
        pulse = pulses(n)

        def row(i, carry):
            hy_behind, hz_behind = carry
            at_x = first_x + i
            inside = jnp.where((at_x >= 0) & (at_x < total_x), 1.0, 0.0)
            scale = in_y * inside
            ex, ey, ez = field[i, 0], field[i, 1], field[i, 2]
            hx, hy, hz = field[i, 3], field[i, 4], field[i, 5]
            ey_on, ez_on = field[i + 1, 1], field[i + 1, 2]
            hx = hx - scale * ((next_y(ez) - ez) - (next_z(ey) - ey))
            hy = hy - scale * ((next_z(ex) - ex) - (ez_on - ez))
            hz = hz - scale * ((ey_on - ey) - (next_y(ex) - ex))
            energy = ex * ex + ey * ey + ez * ez
            factor = scale / (coef[i, 0] + coef[i, 1] * energy)
            ex = ex + factor * ((hz - prev_y(hz)) - (hy - prev_z(hy))) + coef[i, 2] * pulse
            ey = ey + factor * ((hx - prev_z(hx)) - (hz - hz_behind))
            ez = ez + factor * ((hy - hy_behind) - (hx - prev_y(hx)))
            field[i, 0], field[i, 1], field[i, 2] = ex, ey, ez
            field[i, 3], field[i, 4], field[i, 5] = hx, hy, hz
            hist[0, n, i] = ex[SUBS:]
            hist[1, n, i] = ey[SUBS:]
            return hy, hz

        zero = jnp.zeros((depth, LANES), jnp.float32)
        lax.fori_loop(n, span - 1 - n, row, (zero, zero))
        return 0

    def pulses(n):
        value = jnp.float32(0.0)
        for m in range(STEPS):
            value = jnp.where(n == m, jnp.float32(drive_at(m)), value)
        return value

    lax.fori_loop(0, STEPS, step, 0)

    pairs = rows // 2
    subs_mine = pl.ds(pl.multiple_of(core * SUBS, SUBS), SUBS)
    subs_theirs = pl.ds(pl.multiple_of((1 - core) * SUBS, SUBS), SUBS)

    def pack(r, _):
        for a in range(6):
            for out, subs in ((mine_out, subs_mine), (send_out, subs_theirs)):
                first = pltpu.roll(field[halo + r, a, subs, :], LANES - halo, 1)
                second = pltpu.roll(field[halo + pairs + r, a, subs, :], half - halo, 1)
                out[r, a] = jnp.where(lane < half, first, second)
        return 0

    lax.fori_loop(0, pairs, pack, 0)

    for r0 in range(0, rows, SUBS):
        sums = [[[None, None], [None, None]] for _ in OMEGAS]
        for c in range(2):
            for n in range(STEPS):
                plane = hist[c, n, pl.ds(halo + r0, SUBS), SUBS - 1, :]
                trig = trig_of(n)
                for f in range(len(OMEGAS)):
                    for part in range(2):
                        term = trig[f][part] * plane
                        before = sums[f][part][c]
                        sums[f][part][c] = term if before is None else before + term
        for f in range(len(OMEGAS)):
            for part in range(2):
                first = pltpu.roll(sums[f][part][0], LANES - halo, 1)
                second = pltpu.roll(sums[f][part][1], half - halo, 1)
                spec_out[2 * f + part, pl.ds(r0, SUBS), :] = jnp.where(lane < half, first, second)


def drive_at(step):
    middle = step + 0.5
    return SOURCE_AMP * (math.sin(OMEGAS[0] * middle) + math.sin(OMEGAS[1] * middle))


def join_body(pos, mine, theirs, *pieces):
    _, member, core = pos()
    lane = lane_iota()
    half = LANES // 2
    width_x = pieces[0].shape[0]
    pairs = mine.shape[0]
    for j in range(GROUP):
        block = member ^ j
        high = block * width_x >= pairs
        base = block * width_x - jnp.where(high, pairs, 0)
        for r in range(width_x):
            for a in range(6):
                one, two = mine[base + r, a], theirs[base + r, a]
                first = jnp.where(core == 0, one, two)
                second = jnp.where(core == 0, two, one)
                low_rows = jnp.where(lane < half, first, pltpu.roll(second, half, 1))
                high_rows = jnp.where(lane < half, pltpu.roll(first, half, 1), second)
                pieces[j][r, a] = jnp.where(high, high_rows, low_rows)


def unquarter_body(pos, p0, p1, p2, p3, out):
    _, member, _ = pos()
    for j, piece in enumerate((p0, p1, p2, p3)):
        cols = pl.ds(pl.multiple_of((member ^ j) * LANES, LANES), LANES)
        for r in range(piece.shape[0]):
            for a in range(6):
                out[a, r, :, cols] = piece[r, a]


def chirp_parts(gap, quarter, length):
    squared = gap * gap
    wrapped = quarter * squared % (8 * length)
    phase = wrapped.astype(jnp.float32) * (math.pi / (4.0 * length))
    scale = 1.0 / math.sqrt(length)
    return jnp.cos(phase) * scale, jnp.sin(phase) * scale


def dot(a, b):
    return lax.dot_general(
        a, b, (((1,), (0,)), ((), ())), precision=HIGHEST, preferred_element_type=jnp.float32
    )


def row_transform_body(chirp_x, *refs):
    pieces, outs = refs[: len(refs) - GROUP], refs[len(refs) - GROUP :]
    for f in range(len(OMEGAS)):
        real = jnp.concatenate([piece[2 * f] for piece in pieces], axis=0)
        imag = jnp.concatenate([piece[2 * f + 1] for piece in pieces], axis=0)
        both = jnp.concatenate([real, imag], axis=1)
        by_real = dot(chirp_x[f, 0], both)
        by_imag = dot(chirp_x[f, 1], both)
        out_real = by_real[:, :LANES] - by_imag[:, LANES:]
        out_imag = by_real[:, LANES:] + by_imag[:, :LANES]
        for j in range(GROUP):
            outs[j][2 * f] = out_real[j * SUBS : (j + 1) * SUBS]
            outs[j][2 * f + 1] = out_imag[j * SUBS : (j + 1) * SUBS]


def stack_body(p0, p1, p2, p3, out):
    for j, piece in enumerate((p0, p1, p2, p3)):
        out[j] = piece[...]


def column_transform_body(chirp_y, mine, theirs, out):
    half = LANES // 2
    lane = lane_iota()
    width_x = out.shape[0]
    for f in range(len(OMEGAS)):
        rows = []
        for part in range(2):
            for c in range(2):
                tiles = []
                for source in (mine, theirs):
                    for j in range(0, GROUP, 2):
                        one, two = source[j, 2 * f + part], source[j + 1, 2 * f + part]
                        if c == 0:
                            tiles.append(jnp.where(lane < half, one, pltpu.roll(two, half, 1)))
                        else:
                            tiles.append(jnp.where(lane < half, pltpu.roll(one, half, 1), two))
                rows.append(jnp.concatenate(tiles, axis=1))
        left = jnp.concatenate(rows, axis=0)
        by_real = dot(left, chirp_y[f, 0])
        by_imag = dot(left, chirp_y[f, 1])
        mid = 2 * SUBS
        out_real = by_real[:mid] - by_imag[mid:]
        out_imag = by_imag[:mid] + by_real[mid:]
        for c in range(2):
            for r in range(width_x):
                out[r, pl.ds(4 * f + 2 * c, 1), :] = out_real[c * SUBS + r : c * SUBS + r + 1]
                out[r, pl.ds(4 * f + 2 * c + 1, 1), :] = out_imag[c * SUBS + r : c * SUBS + r + 1]


def shift_xor(array, by):
    count = lax.axis_size("lat")
    return lax.ppermute(array, "lat", [(i, i ^ by) for i in range(count)])


def swap_cores(array):
    return lax.ppermute(array, "depth", [(0, 1), (1, 0)])


def local_regrouped(fields, material, source_mask, eps_table, kerr_table):
    width_x = fields.shape[1]
    lat_count = lax.axis_size("lat")
    groups = lat_count // GROUP
    rows = GROUP * width_x
    total_x = width_x * lat_count
    span_y = fields.shape[3]
    group, member, core = place()

    pieces = call(
        functools.partial(quarters_body, place),
        [f32(width_x, 10, SUBS, LANES)] * GROUP,
        (fields, material, source_mask),
        name="quarters",
    )
    pieces = [pieces[0]] + [shift_xor(pieces[j], j) for j in range(1, GROUP)]

    j_of = jnp.arange(GROUP * SUBS, dtype=jnp.int32) // SUBS
    r_of = jnp.arange(GROUP * SUBS, dtype=jnp.int32) % SUBS
    x_out = group * rows + (member ^ j_of) * width_x + r_of
    k_of = jnp.arange(total_x, dtype=jnp.int32)
    x_in = (group ^ (k_of // rows)) * rows + k_of % rows
    x_gap = x_out[:, None] - x_in[None, :]
    chirp_x = jnp.stack([jnp.stack(chirp_parts(x_gap, q, total_x)) for q in QUARTERS])
    half = LANES // 2
    col_count = span_y // 2
    k_of = jnp.arange(span_y, dtype=jnp.int32)
    source = k_of // (GROUP * half)
    y_in = (
        LANES * (member ^ (k_of // half % GROUP)) + half * (core ^ source) + k_of % half
    )
    y_out = core * col_count + jnp.arange(col_count, dtype=jnp.int32)
    y_gap = y_in[:, None] - y_out[None, :]
    chirp_y = jnp.stack([jnp.stack(chirp_parts(y_gap, q, span_y)) for q in QUARTERS])

    own, up, down = call(
        functools.partial(gather_rows_body, place),
        [f32(rows, 10, SUBS, LANES), f32(STEPS, 10, SUBS, LANES), f32(STEPS, 10, SUBS, LANES)],
        pieces,
        name="gather_rows",
    )
    upward = [(i, i + GROUP) for i in range(lat_count - GROUP)]
    low = lax.ppermute(up, "lat", upward)
    high = lax.ppermute(down, "lat", [(b, a) for a, b in upward])
    theirs = swap_cores(
        call(functools.partial(windows_body, place), f32(rows, 8, SUBS, LANES), (own,), name="win")
    )
    theirs_halo = swap_cores(
        call(
            functools.partial(windows2_body, place),
            f32(2 * STEPS, 8, SUBS, LANES),
            (low, high),
            name="win_halo",
        )
    )
    span = rows + 2 * STEPS
    mine, send, spec = call(
        functools.partial(steps_body, place, total_x, span_y),
        [
            f32(rows // 2, 6, SUBS, LANES),
            f32(rows // 2, 6, SUBS, LANES),
            f32(4, rows, LANES),
        ],
        (eps_table, kerr_table, own, low, high, theirs, theirs_halo),
        in_specs=[SMEM, SMEM] + [VMEM] * 5,
        scratch=[
            pltpu.VMEM((span, 6, 2 * SUBS, LANES), jnp.float32),
            pltpu.VMEM((span, 3, 2 * SUBS, LANES), jnp.float32),
            pltpu.VMEM((2, STEPS, span, SUBS, LANES), jnp.float32),
        ],
        name="steps",
    )
    specs = [spec] + [shift_xor(spec, GROUP * k) for k in range(1, groups)]
    joined = call(
        functools.partial(join_body, place),
        [f32(width_x, 6, SUBS, LANES)] * GROUP,
        (mine, swap_cores(send)),
        name="join",
    )
    joined = [joined[0]] + [shift_xor(joined[j], j) for j in range(1, GROUP)]
    turned = call(row_transform_body, [f32(4, SUBS, LANES)] * GROUP, [chirp_x] + specs, name="rowt")
    turned = [turned[0]] + [shift_xor(turned[j], j) for j in range(1, GROUP)]
    stacked = call(stack_body, f32(GROUP, 4, SUBS, LANES), turned, name="stack")
    image = call(
        column_transform_body,
        f32(width_x, 8, col_count),
        (chirp_y, stacked, swap_cores(stacked)),
        name="colt",
    )
    state = call(
        functools.partial(unquarter_body, place),
        f32(6, width_x, SUBS, span_y),
        joined,
        name="unquarter",
    )
    return state, image


def can_regroup(fields, eps_table):
    lat_count = lax.axis_size("lat")
    groups = lat_count // GROUP
    return (
        lax.axis_size("depth") == 2
        and lat_count % GROUP == 0
        and groups & (groups - 1) == 0
        and fields.shape[1] <= SUBS
        and (GROUP * fields.shape[1]) % SUBS == 0
        and GROUP * fields.shape[1] >= STEPS
        and fields.shape[2] == SUBS
        and fields.shape[3] == GROUP * LANES
    )


def local(fields, material, source_mask, eps_table, kerr_table):
    run = local_regrouped if can_regroup(fields, eps_table) else local_general
    return run(fields, material, source_mask, eps_table, kerr_table)


def solution(mesh):
    placed = (
        P(None, "lat", "depth", None),
        P("lat", "depth", None),
        P("lat", "depth", None),
        P(),
        P(),
    )
    return jax.shard_map(
        local,
        mesh=mesh,
        in_specs=placed,
        out_specs=(P(None, "lat", "depth", None), P("lat", None, "depth")),
        check_vma=False,
    )
```

```python
import functools
import math

import jax
import jax.numpy as jnp
from jax import lax
from jax.experimental import pallas as pl
from jax.experimental.pallas import tpu as pltpu
from jax.sharding import PartitionSpec as P

STEPS = 16
HALO_STEPS = 4


COURANT = 0.55
OMEGAS = (0.9, 1.3)
SOURCE_AMP = 1.0
QUARTERS = (3, 5)
HIGHEST = lax.Precision.HIGHEST


def padded_2(block, sides, width):
    for axis, dim in sides:
        count = lax.axis_size(axis)
        forward = [(i, i + 1) for i in range(count - 1)]
        backward = [(target, source) for source, target in forward]
        low = lax.ppermute(
            lax.slice_in_dim(block, block.shape[dim] - width, None, axis=dim), axis, forward
        )
        high = lax.ppermute(lax.slice_in_dim(block, 0, width, axis=dim), axis, backward)
        block = jnp.concatenate([low, block, high], axis=dim)
    return block


def from_root(block, axis, owner):
    block = jnp.where(lax.axis_index(axis) == owner, block, jnp.zeros_like(block))
    return lax.psum(block, axis)


def forward_diff(field, along):
    length = field.shape[along]
    ahead = lax.slice_in_dim(field, 1, length, axis=along)
    ahead = jnp.concatenate(
        [ahead, jnp.zeros_like(lax.slice_in_dim(field, 0, 1, axis=along))], axis=along
    )
    return ahead - field


def backward_diff(field, along):
    length = field.shape[along]
    behind = lax.slice_in_dim(field, 0, length - 1, axis=along)
    behind = jnp.concatenate(
        [jnp.zeros_like(lax.slice_in_dim(field, 0, 1, axis=along)), behind], axis=along
    )
    return field - behind


def drive(moment):
    middle = moment + 0.5
    return SOURCE_AMP * (jnp.sin(OMEGAS[0] * middle) + jnp.sin(OMEGAS[1] * middle))


def yee_step(fields, permittivity, kerr_coef, source_flag, inside, pulse):
    elec_x, elec_y, elec_z = (fields[0], fields[1], fields[2])
    magn_x, magn_y, magn_z = (fields[3], fields[4], fields[5])
    magn_x = (magn_x - COURANT * (forward_diff(elec_z, 2) - forward_diff(elec_y, 1))) * inside
    magn_y = (magn_y - COURANT * (forward_diff(elec_x, 1) - forward_diff(elec_z, 0))) * inside
    magn_z = (magn_z - COURANT * (forward_diff(elec_y, 0) - forward_diff(elec_x, 2))) * inside
    energy = elec_x * elec_x + elec_y * elec_y + elec_z * elec_z
    factor = COURANT / (permittivity + kerr_coef * energy)
    new_x = (
        elec_x
        + factor * (backward_diff(magn_z, 2) - backward_diff(magn_y, 1))
        + source_flag * pulse
    ) * inside
    new_y = (elec_y + factor * (backward_diff(magn_x, 1) - backward_diff(magn_z, 0))) * inside
    new_z = (elec_z + factor * (backward_diff(magn_y, 0) - backward_diff(magn_x, 2))) * inside
    return jnp.stack([new_x, new_y, new_z, magn_x, magn_y, magn_z])


def lookup(material, table):
    result = jnp.zeros(material.shape, jnp.float32)
    for level in range(table.shape[0]):
        result = jnp.where(material == level, table[level], result)
    return result


def accumulate(spectrum, plane, moment):
    later = moment + 1.0
    trig = jnp.stack(
        [jnp.stack([jnp.cos(omega * later), -jnp.sin(omega * later)]) for omega in OMEGAS]
    )
    return spectrum + trig[:, None, :, None, None] * plane[None, :, None, :, :]


def chirp(row_index, col_index, length):
    gap = row_index[:, None] - col_index[None, :]
    squared = gap * gap
    reals, imags = ([], [])
    for quarter in QUARTERS:
        wrapped = quarter * squared % (8 * length)
        phase = wrapped.astype(jnp.float32) * (math.pi / (4.0 * length))
        reals.append(jnp.cos(phase) / math.sqrt(length))
        imags.append(jnp.sin(phase) / math.sqrt(length))
    return (jnp.stack(reals), jnp.stack(imags))


def column_transform(real, imag, y_real, y_imag):
    v_real = jnp.einsum("fcxy,fyk->fcxk", real, y_real, precision=HIGHEST) - jnp.einsum(
        "fcxy,fyk->fcxk", imag, y_imag, precision=HIGHEST
    )
    v_imag = jnp.einsum("fcxy,fyk->fcxk", real, y_imag, precision=HIGHEST) + jnp.einsum(
        "fcxy,fyk->fcxk", imag, y_real, precision=HIGHEST
    )
    return (v_real, v_imag)


def row_transform(x_real, x_imag, v_real, v_imag):
    w_real = jnp.einsum("fix,fcxk->ifck", x_real, v_real, precision=HIGHEST) - jnp.einsum(
        "fix,fcxk->ifck", x_imag, v_imag, precision=HIGHEST
    )
    w_imag = jnp.einsum("fix,fcxk->ifck", x_real, v_imag, precision=HIGHEST) + jnp.einsum(
        "fix,fcxk->ifck", x_imag, v_real, precision=HIGHEST
    )
    return jnp.stack([w_real, w_imag], axis=3)


def local_general(fields, material, source_mask, eps_table, kerr_table):
    width_x = fields.shape[1]
    depth_z = fields.shape[2]
    span_y = fields.shape[3]
    lat_count = lax.axis_size("lat")
    depth_count = lax.axis_size("depth")
    total_x = width_x * lat_count
    total_z = depth_z * depth_count
    lat_pos = lax.axis_index("lat")
    depth_pos = lax.axis_index("depth")
    coefs = jnp.stack(
        [lookup(material, eps_table), lookup(material, kerr_table), source_mask.astype(jnp.float32)]
    )
    empty_spectrum = jnp.zeros((2, 2, 2, width_x, span_y), jnp.float32)
    coef_pad = padded_2(coefs, (("depth", 2), ("lat", 1)), HALO_STEPS)
    place_x = lat_pos * width_x - HALO_STEPS + jnp.arange(width_x + 2 * HALO_STEPS, dtype=jnp.int32)
    place_z = (
        depth_pos * depth_z - HALO_STEPS + jnp.arange(depth_z + 2 * HALO_STEPS, dtype=jnp.int32)
    )
    valid_x = (place_x >= 0) & (place_x < total_x)
    valid_z = (place_z >= 0) & (place_z < total_z)
    valid = valid_x[:, None] & valid_z[None, :]
    setup_inside = valid.astype(jnp.float32)[:, :, None]
    setup_permittivity = jnp.where(valid[:, :, None], coef_pad[0], 1.0)
    kerr_coef = coef_pad[1]
    source_flag = coef_pad[2]

    def one_block(block, carry):
        state, spectrum = carry
        padded = padded_2(state, (("depth", 2), ("lat", 1)), HALO_STEPS)
        for inner in range(HALO_STEPS):
            moment = (block * HALO_STEPS + inner).astype(jnp.float32)
            padded = yee_step(
                padded, setup_permittivity, kerr_coef, source_flag, setup_inside, drive(moment)
            )
            plane = padded[0:2, HALO_STEPS : HALO_STEPS + width_x, HALO_STEPS + depth_z - 1, :]
            spectrum = accumulate(spectrum, plane, moment)
        state = padded[:, HALO_STEPS : HALO_STEPS + width_x, HALO_STEPS : HALO_STEPS + depth_z]
        return (state, spectrum)

    state, spectrum = lax.fori_loop(0, STEPS // HALO_STEPS, one_block, (fields, empty_spectrum))
    spectrum = from_root(spectrum, "depth", depth_count - 1)
    col_count = span_y // depth_count
    col_index = depth_pos * col_count + jnp.arange(col_count, dtype=jnp.int32)
    y_real, y_imag = chirp(jnp.arange(span_y, dtype=jnp.int32), col_index, span_y)
    v_real, v_imag = column_transform(spectrum[:, :, 0], spectrum[:, :, 1], y_real, y_imag)
    row_local = lat_pos * width_x + jnp.arange(width_x, dtype=jnp.int32)
    row_index = jnp.arange(width_x * lax.axis_size("lat"), dtype=jnp.int32)
    x_real, x_imag = chirp(row_index, row_local, total_x)
    image = lax.psum_scatter(
        row_transform(x_real, x_imag, v_real, v_imag), "lat", scatter_dimension=0, tiled=True
    )
    return (state, image.reshape(width_x, 8, col_count))


GROUP = 4
LANES = 128
SUBS = 8
PER_TILE = 4
UNROLL = 8
VMEM = pl.BlockSpec(memory_space=pltpu.VMEM)
SMEM = pl.BlockSpec(memory_space=pltpu.SMEM)


def place():
    lat_pos = lax.axis_index("lat")
    return lat_pos // GROUP, lat_pos % GROUP, lax.axis_index("depth")


def call(body, out_shape, operands, in_specs=None, scratch=(), name=None, near=True):
    if near:
        specs = in_specs or [VMEM] * len(operands)
        operands = [
            pltpu.with_memory_space_constraint(operand, pltpu.VMEM) if spec is VMEM else operand
            for operand, spec in zip(operands, specs)
        ]
    return pl.pallas_call(
        body,
        out_shape=out_shape,
        in_specs=in_specs or [VMEM] * len(operands),
        out_specs=[VMEM] * len(out_shape) if isinstance(out_shape, list) else VMEM,
        scratch_shapes=list(scratch),
        compiler_params=pltpu.CompilerParams(vmem_limit_bytes=56 * 1024 * 1024),
        name=name,
    )(*operands)


def f32(*shape):
    return pltpu.VMEM(shape, jnp.float32)


def final(*shape):
    return jax.ShapeDtypeStruct(shape, jnp.float32)


def lane_iota(rows=SUBS):
    return lax.broadcasted_iota(jnp.int32, (rows, LANES), 1)


def quarters_body(pos, fields, material, mask, *pieces):
    width_x = fields.shape[1]
    lane = lane_iota()
    _, member, _ = pos()
    halo = STEPS

    def row(r, _):
        for j in range(GROUP):
            quarter = member ^ j
            left = jnp.maximum(quarter - 1, 0)
            right = jnp.minimum(quarter + 1, GROUP - 1)
            has_left = jnp.where(quarter > 0, 1.0, 0.0)
            has_right = jnp.where(quarter < GROUP - 1, 1.0, 0.0)
            keep = jnp.where(lane >= LANES // 2, has_left, has_right)

            def read(a, block):
                cols = pl.ds(pl.multiple_of(block * LANES, LANES), LANES)
                if a < 6:
                    return fields[a, r, :, cols]
                source = material if a == 6 else mask
                return source[r, :, cols].astype(jnp.float32)

            for g in range(8 // PER_TILE):
                packed = jnp.zeros((SUBS, LANES), jnp.float32)
                for k in range(PER_TILE):
                    a = g * PER_TILE + k
                    pieces[j][r, a] = read(a, quarter)
                    edge = jnp.where(lane >= LANES // 2, read(a, left), read(a, right)) * keep
                    edge = pltpu.roll(edge, (2 * halo * k + halo) % LANES, 1)
                    packed = jnp.where(lane // (2 * halo) == k, edge, packed)
                pieces[j][r, 8 + g] = packed
        return 0

    lax.fori_loop(0, width_x, row, 0)


def gather_rows_body(pos, p0, p1, p2, p3, own, up, down):
    _, member, _ = pos()
    width_x = p0.shape[0]
    rows = GROUP * width_x
    for j, piece in enumerate((p0, p1, p2, p3)):
        first = (member ^ j) * width_x
        for r in range(width_x):
            own[first + r] = piece[r]
    for r in range(STEPS):
        up[r] = own[rows - STEPS + r]
        down[r] = own[r]


def window_tile(packed, r, a, core, lane):
    half = LANES // 2
    halo = STEPS
    main = pltpu.roll(packed[r, a], (halo + half * core) % LANES, 1)
    edge = pltpu.roll(
        packed[r, 8 + a // PER_TILE], (half * core + LANES - 2 * halo * (a % PER_TILE)) % LANES, 1
    )
    below = jnp.where(core == 0, halo, 0)
    above = jnp.where(core == 0, LANES, half + halo)
    return jnp.where((lane < below) | (lane >= above), edge, main)


def windows_body(pos, packed, out):
    _, _, core = pos()
    lane = lane_iota()

    def row(r, _):
        for a in range(8):
            out[r, a] = window_tile(packed, r, a, 1 - core, lane)
        return 0

    lax.fori_loop(0, packed.shape[0], row, 0)


def windows2_body(pos, low, high, out):
    _, _, core = pos()
    lane = lane_iota()

    def row(r, _):
        for a in range(8):
            out[r, a] = window_tile(low, r, a, 1 - core, lane)
            out[STEPS + r, a] = window_tile(high, r, a, 1 - core, lane)
        return 0

    lax.fori_loop(0, STEPS, row, 0)


def trig_of(step):
    later = step + 1.0
    return [[math.cos(omega * later), -math.sin(omega * later)] for omega in OMEGAS]


def steps_body(
    pos, total_x, total_y, eps, kerr, own, low, high, theirs, theirs_halo,
    mine_out, send_out, spec_out, field, coef, hist,
):
    group, member, core = pos()
    lane = lane_iota()
    half = LANES // 2
    halo = STEPS
    rows = own.shape[0]
    span = rows + 2 * halo
    depth = 2 * SUBS
    levels = eps.shape[0]

    def put(row, core_at, tiles):
        subs = pl.ds(pl.multiple_of(core_at * SUBS, SUBS), SUBS)
        for a in range(6):
            field[row, a, subs, :] = tiles[a]
        eps_of = jnp.zeros((SUBS, LANES), jnp.float32)
        kerr_of = jnp.zeros((SUBS, LANES), jnp.float32)
        for level in range(levels):
            hit = tiles[6] == float(level)
            eps_of = jnp.where(hit, eps[level], eps_of)
            kerr_of = jnp.where(hit, kerr[level], kerr_of)
        coef[row, 0, subs, :] = eps_of
        coef[row, 1, subs, :] = kerr_of
        coef[row, 2, subs, :] = tiles[7]

    def fill(packed, at, count, other, other_at):
        def row(r, _):
            put(at + r, core, [window_tile(packed, r, a, core, lane) for a in range(8)])
            put(at + r, 1 - core, [other[other_at + r, a] for a in range(8)])
            return 0

        lax.fori_loop(0, count, row, 0)

    fill(own, halo, rows, theirs, 0)
    fill(low, 0, halo, theirs_halo, 0)
    fill(high, halo + rows, halo, theirs_halo, halo)

    lane2 = lane_iota(depth)
    at_y = member * LANES + core * half - halo + lane2
    in_y = jnp.where((at_y >= 0) & (at_y < total_y), COURANT, 0.0)

    def next_y(f):
        return pltpu.roll(f, LANES - 1, 1)

    def prev_y(f):
        return pltpu.roll(f, 1, 1)

    sub = lax.broadcasted_iota(jnp.int32, (SUBS, LANES), 0)

    def next_z(f):
        low, high = pltpu.roll(f[:SUBS], SUBS - 1, 0), pltpu.roll(f[SUBS:], SUBS - 1, 0)
        return jnp.concatenate(
            [jnp.where(sub < SUBS - 1, low, high), jnp.where(sub < SUBS - 1, high, 0.0)], axis=0
        )

    def prev_z(f):
        low, high = pltpu.roll(f[:SUBS], 1, 0), pltpu.roll(f[SUBS:], 1, 0)
        return jnp.concatenate(
            [jnp.where(sub > 0, low, 0.0), jnp.where(sub > 0, high, low)], axis=0
        )

    first_x = group * rows - halo

    def step(n, _):
        pulse = pulses(n)

        def rows_at(b, carry):
            hy_behind, hz_behind = carry
            first = n + b * UNROLL
            at = [first + u for u in range(UNROLL)]
            old = [[field[i, a] for a in range(6)] for i in at]
            ahead = [None, field[first + UNROLL, 1], field[first + UNROLL, 2]]
            scales = []
            for u, i in enumerate(at):
                at_x = first_x + i
                inside = jnp.where((at_x >= 0) & (at_x < total_x), 1.0, 0.0)
                scales.append(in_y * inside)
            for u, i in enumerate(at):
                ex, ey, ez, hx, hy, hz = old[u]
                on = old[u + 1] if u + 1 < UNROLL else ahead
                scale = scales[u]
                hx = hx - scale * ((next_y(ez) - ez) - (next_z(ey) - ey))
                hy = hy - scale * ((next_z(ex) - ex) - (on[2] - ez))
                hz = hz - scale * ((on[1] - ey) - (next_y(ex) - ex))
                energy = ex * ex + ey * ey + ez * ez
                factor = scale / (coef[i, 0] + coef[i, 1] * energy)
                ex = ex + factor * ((hz - prev_y(hz)) - (hy - prev_z(hy))) + coef[i, 2] * pulse
                ey = ey + factor * ((hx - prev_z(hx)) - (hz - hz_behind))
                ez = ez + factor * ((hy - hy_behind) - (hx - prev_y(hx)))
                field[i, 0], field[i, 1], field[i, 2] = ex, ey, ez
                field[i, 3], field[i, 4], field[i, 5] = hx, hy, hz
                hist[0, n, i] = ex[SUBS:]
                hist[1, n, i] = ey[SUBS:]
                hy_behind, hz_behind = hy, hz
            return hy_behind, hz_behind

        zero = jnp.zeros((depth, LANES), jnp.float32)
        count = span - 1 - 2 * n
        lax.fori_loop(0, (count + UNROLL - 1) // UNROLL, rows_at, (zero, zero))
        return 0

    def pulses(n):
        value = jnp.float32(0.0)
        for m in range(STEPS):
            value = jnp.where(n == m, jnp.float32(drive_at(m)), value)
        return value

    lax.fori_loop(0, STEPS, step, 0)

    pairs = rows // 2
    subs_mine = pl.ds(pl.multiple_of(core * SUBS, SUBS), SUBS)
    subs_theirs = pl.ds(pl.multiple_of((1 - core) * SUBS, SUBS), SUBS)

    def pack(r, _):
        for a in range(6):
            for out, subs in ((mine_out, subs_mine), (send_out, subs_theirs)):
                first = pltpu.roll(field[halo + r, a, subs, :], LANES - halo, 1)
                second = pltpu.roll(field[halo + pairs + r, a, subs, :], half - halo, 1)
                out[r, a] = jnp.where(lane < half, first, second)
        return 0

    lax.fori_loop(0, pairs, pack, 0)

    for r0 in range(0, rows, SUBS):
        sums = [[[None, None], [None, None]] for _ in OMEGAS]
        for c in range(2):
            for n in range(STEPS):
                plane = hist[c, n, pl.ds(halo + r0, SUBS), SUBS - 1, :]
                trig = trig_of(n)
                for f in range(len(OMEGAS)):
                    for part in range(2):
                        term = trig[f][part] * plane
                        before = sums[f][part][c]
                        sums[f][part][c] = term if before is None else before + term
        for f in range(len(OMEGAS)):
            for part in range(2):
                first = pltpu.roll(sums[f][part][0], LANES - halo, 1)
                second = pltpu.roll(sums[f][part][1], half - halo, 1)
                spec_out[2 * f + part, pl.ds(r0, SUBS), :] = jnp.where(lane < half, first, second)


def drive_at(step):
    middle = step + 0.5
    return SOURCE_AMP * (math.sin(OMEGAS[0] * middle) + math.sin(OMEGAS[1] * middle))


def join_body(pos, mine, theirs, *pieces):
    _, member, core = pos()
    lane = lane_iota()
    half = LANES // 2
    width_x = pieces[0].shape[0]
    pairs = mine.shape[0]
    for j in range(GROUP):
        block = member ^ j
        high = block * width_x >= pairs
        base = block * width_x - jnp.where(high, pairs, 0)
        for r in range(width_x):
            for a in range(6):
                one, two = mine[base + r, a], theirs[base + r, a]
                first = jnp.where(core == 0, one, two)
                second = jnp.where(core == 0, two, one)
                low_rows = jnp.where(lane < half, first, pltpu.roll(second, half, 1))
                high_rows = jnp.where(lane < half, pltpu.roll(first, half, 1), second)
                pieces[j][r, a] = jnp.where(high, high_rows, low_rows)


def unquarter_body(pos, p0, p1, p2, p3, out):
    _, member, _ = pos()
    for j, piece in enumerate((p0, p1, p2, p3)):
        cols = pl.ds(pl.multiple_of((member ^ j) * LANES, LANES), LANES)
        for r in range(piece.shape[0]):
            for a in range(6):
                out[a, r, :, cols] = piece[r, a]


def chirp_parts(gap, quarter, length):
    squared = gap * gap
    wrapped = quarter * squared % (8 * length)
    phase = wrapped.astype(jnp.float32) * (math.pi / (4.0 * length))
    scale = 1.0 / math.sqrt(length)
    return jnp.cos(phase) * scale, jnp.sin(phase) * scale


def dot(a, b):
    return lax.dot_general(
        a, b, (((1,), (0,)), ((), ())), precision=HIGHEST, preferred_element_type=jnp.float32
    )


def row_transform_body(chirp_x, *refs):
    pieces, outs = refs[: len(refs) - GROUP], refs[len(refs) - GROUP :]
    for f in range(len(OMEGAS)):
        real = jnp.concatenate([piece[2 * f] for piece in pieces], axis=0)
        imag = jnp.concatenate([piece[2 * f + 1] for piece in pieces], axis=0)
        both = jnp.concatenate([real, imag], axis=1)
        by_real = dot(chirp_x[f, 0], both)
        by_imag = dot(chirp_x[f, 1], both)
        out_real = by_real[:, :LANES] - by_imag[:, LANES:]
        out_imag = by_real[:, LANES:] + by_imag[:, :LANES]
        for j in range(GROUP):
            outs[j][2 * f] = out_real[j * SUBS : (j + 1) * SUBS]
            outs[j][2 * f + 1] = out_imag[j * SUBS : (j + 1) * SUBS]


def stack_body(p0, p1, p2, p3, out):
    for j, piece in enumerate((p0, p1, p2, p3)):
        out[j] = piece[...]


def column_transform_body(chirp_y, mine, theirs, out):
    half = LANES // 2
    lane = lane_iota()
    width_x = out.shape[0]
    for f in range(len(OMEGAS)):
        rows = []
        for part in range(2):
            for c in range(2):
                tiles = []
                for source in (mine, theirs):
                    for j in range(0, GROUP, 2):
                        one, two = source[j, 2 * f + part], source[j + 1, 2 * f + part]
                        if c == 0:
                            tiles.append(jnp.where(lane < half, one, pltpu.roll(two, half, 1)))
                        else:
                            tiles.append(jnp.where(lane < half, pltpu.roll(one, half, 1), two))
                rows.append(jnp.concatenate(tiles, axis=1))
        left = jnp.concatenate(rows, axis=0)
        by_real = dot(left, chirp_y[f, 0])
        by_imag = dot(left, chirp_y[f, 1])
        mid = 2 * SUBS
        out_real = by_real[:mid] - by_imag[mid:]
        out_imag = by_imag[:mid] + by_real[mid:]
        for c in range(2):
            for r in range(width_x):
                out[r, pl.ds(4 * f + 2 * c, 1), :] = out_real[c * SUBS + r : c * SUBS + r + 1]
                out[r, pl.ds(4 * f + 2 * c + 1, 1), :] = out_imag[c * SUBS + r : c * SUBS + r + 1]


def shift_xor(array, by):
    count = lax.axis_size("lat")
    return lax.ppermute(array, "lat", [(i, i ^ by) for i in range(count)])


def swap_cores(array):
    return lax.ppermute(array, "depth", [(0, 1), (1, 0)])


def local_regrouped(fields, material, source_mask, eps_table, kerr_table):
    width_x = fields.shape[1]
    lat_count = lax.axis_size("lat")
    groups = lat_count // GROUP
    rows = GROUP * width_x
    total_x = width_x * lat_count
    span_y = fields.shape[3]
    group, member, core = place()

    pieces = call(
        functools.partial(quarters_body, place),
        [f32(width_x, 10, SUBS, LANES)] * GROUP,
        (fields, material, source_mask),
        name="quarters",
        near=False,
    )
    pieces = [pieces[0]] + [shift_xor(pieces[j], j) for j in range(1, GROUP)]

    j_of = jnp.arange(GROUP * SUBS, dtype=jnp.int32) // SUBS
    r_of = jnp.arange(GROUP * SUBS, dtype=jnp.int32) % SUBS
    x_out = group * rows + (member ^ j_of) * width_x + r_of
    k_of = jnp.arange(total_x, dtype=jnp.int32)
    x_in = (group ^ (k_of // rows)) * rows + k_of % rows
    x_gap = x_out[:, None] - x_in[None, :]
    chirp_x = jnp.stack([jnp.stack(chirp_parts(x_gap, q, total_x)) for q in QUARTERS])
    half = LANES // 2
    col_count = span_y // 2
    k_of = jnp.arange(span_y, dtype=jnp.int32)
    source = k_of // (GROUP * half)
    y_in = (
        LANES * (member ^ (k_of // half % GROUP)) + half * (core ^ source) + k_of % half
    )
    y_out = core * col_count + jnp.arange(col_count, dtype=jnp.int32)
    y_gap = y_in[:, None] - y_out[None, :]
    chirp_y = jnp.stack([jnp.stack(chirp_parts(y_gap, q, span_y)) for q in QUARTERS])

    own, up, down = call(
        functools.partial(gather_rows_body, place),
        [f32(rows, 10, SUBS, LANES), f32(STEPS, 10, SUBS, LANES), f32(STEPS, 10, SUBS, LANES)],
        pieces,
        name="gather_rows",
    )
    upward = [(i, i + GROUP) for i in range(lat_count - GROUP)]
    low = lax.ppermute(up, "lat", upward)
    high = lax.ppermute(down, "lat", [(b, a) for a, b in upward])
    theirs = swap_cores(
        call(functools.partial(windows_body, place), f32(rows, 8, SUBS, LANES), (own,), name="win")
    )
    theirs_halo = swap_cores(
        call(
            functools.partial(windows2_body, place),
            f32(2 * STEPS, 8, SUBS, LANES),
            (low, high),
            name="win_halo",
        )
    )
    span = rows + 2 * STEPS
    mine, send, spec = call(
        functools.partial(steps_body, place, total_x, span_y),
        [
            f32(rows // 2, 6, SUBS, LANES),
            f32(rows // 2, 6, SUBS, LANES),
            f32(4, rows, LANES),
        ],
        (eps_table, kerr_table, own, low, high, theirs, theirs_halo),
        in_specs=[SMEM, SMEM] + [VMEM] * 5,
        scratch=[
            pltpu.VMEM((span + UNROLL, 6, 2 * SUBS, LANES), jnp.float32),
            pltpu.VMEM((span + UNROLL, 3, 2 * SUBS, LANES), jnp.float32),
            pltpu.VMEM((2, STEPS, span + UNROLL, SUBS, LANES), jnp.float32),
        ],
        name="steps",
    )
    specs = [spec] + [shift_xor(spec, GROUP * k) for k in range(1, groups)]
    joined = call(
        functools.partial(join_body, place),
        [f32(width_x, 6, SUBS, LANES)] * GROUP,
        (mine, swap_cores(send)),
        name="join",
    )
    joined = [joined[0]] + [shift_xor(joined[j], j) for j in range(1, GROUP)]
    turned = call(row_transform_body, [f32(4, SUBS, LANES)] * GROUP, [chirp_x] + specs, name="rowt")
    turned = [turned[0]] + [shift_xor(turned[j], j) for j in range(1, GROUP)]
    stacked = call(stack_body, f32(GROUP, 4, SUBS, LANES), turned, name="stack")
    image = call(
        column_transform_body,
        final(width_x, 8, col_count),
        (chirp_y, stacked, swap_cores(stacked)),
        name="colt",
    )
    state = call(
        functools.partial(unquarter_body, place),
        final(6, width_x, SUBS, span_y),
        joined,
        name="unquarter",
    )
    return state, image


def can_regroup(fields, eps_table):
    lat_count = lax.axis_size("lat")
    groups = lat_count // GROUP
    return (
        lax.axis_size("depth") == 2
        and lat_count % GROUP == 0
        and groups & (groups - 1) == 0
        and fields.shape[1] <= SUBS
        and (GROUP * fields.shape[1]) % SUBS == 0
        and GROUP * fields.shape[1] >= STEPS
        and fields.shape[2] == SUBS
        and fields.shape[3] == GROUP * LANES
    )


def local(fields, material, source_mask, eps_table, kerr_table):
    run = local_regrouped if can_regroup(fields, eps_table) else local_general
    return run(fields, material, source_mask, eps_table, kerr_table)


def solution(mesh):
    placed = (
        P(None, "lat", "depth", None),
        P("lat", "depth", None),
        P("lat", "depth", None),
        P(),
        P(),
    )
    return jax.shard_map(
        local,
        mesh=mesh,
        in_specs=placed,
        out_specs=(P(None, "lat", "depth", None), P("lat", None, "depth")),
        check_vma=False,
    )
```
